32 devices in a mesh: band: 4 (over y, x), region: 8 (over z, core).
Axes of the slice: x: 2, y: 2, z: 4, core: 2. Of those that a mesh axis runs over, the one named last changes fastest.
Arguments:
- fields: float32 [8192, 512], P(('band', 'region')), may hold values from -6 to 6
- send_list: int32 [4, 8, 4, 2], replicated, may hold values from -1 to 1, as said below
- departure: int32 [16, 8192], P(None, ('band', 'region')), may hold values from 0 to 1279, as said below
- hweight: float32 [16, 8192], P(None, ('band', 'region')), may hold values from -0.2 to 0.5
- base_level: int32 [128, 8192], P(None, ('band', 'region')), may hold values from 1 to 125
- vweight: float32 [4, 128, 8192], P(None, None, ('band', 'region')), may hold values from -0.25 to 0.75
- vertical_op: float32 [128, 128], replicated, may hold values from -0.4 to 2, as said below
Outputs:
- level_shards: float32 [512, 8192], P('region', 'band')
The draws below stay inside these ranges and needn't reach their ends.
Inputs may be any that keep to these rules, and one draw needn't show every extreme that they name: send_list[b, r, d] names distinct block numbers of device (b, r), each block being 128 consecutive points of it; a list holds 1 to 2 numbers followed by -1 in the remaining entries, and in every draw some region's lists are all full. departure[c, p] indexes the extended rows of point p's device: below 256 the device's own point, else 256 + d * 2 * 128 + s for row s of part d; only rows delivered by an existing neighbour from a list entry that is not -1 are named. vertical_op[k, l] is zero where k and l differ by more than 2.
All inputs are finite; a program needn't handle non-finite values.
Results may differ from the reference program's by a relative error of at most 0.0003.
Values sent between devices are 32-bit elements; how exact they have to be, the bound alone decides.
No kernel may reach another device: no remote copies, remote signals or barrier semaphores. Data moves between devices by JAX's collectives and lax.ppermute only.
A program may use at most 64 MiB of HBM per device.

```python
import jax
import jax.numpy as jnp
from jax import lax

LEV = 128
P_DEV = 256
BLK = 128
STENCIL = 16
HB = 2
FL = 512
NPTS = 8192
N_BAND = 4
N_REGION = 8


def halo_counts(key):
    count_key, star_key = jax.random.split(jax.random.fold_in(key, 11))
    counts = jax.random.randint(count_key, (N_BAND, N_REGION, 4), 1, HB + 1)
    star_region = jax.random.randint(star_key, (), 0, N_REGION)
    region_ids = jnp.arange(N_REGION)[None, :, None]
    counts = jnp.where(region_ids == star_region, HB, counts)
    return (counts, star_region)


def draw_send_list(key, part):
    counts, star_region = halo_counts(key)
    order_keys = jax.random.split(jax.random.fold_in(key, 23), N_BAND * N_REGION * 4)
    orders = jax.vmap(lambda one_key: jax.random.permutation(one_key, P_DEV // BLK))(order_keys)
    orders = orders[:, :HB].reshape(N_BAND, N_REGION, 4, HB)
    slot_ids = jnp.arange(HB)[None, None, None, :]
    return jnp.where(slot_ids < counts[..., None], orders, -1).astype(jnp.int32)


def draw_departure(key, part):
    counts, star_region = halo_counts(key)
    band_ids = jnp.arange(N_BAND)[:, None]
    from_prev_band = jnp.where(band_ids > 0, jnp.roll(counts[:, :, 0], 1, axis=0), 0)
    from_next_band = jnp.where(band_ids < N_BAND - 1, jnp.roll(counts[:, :, 1], -1, axis=0), 0)
    from_prev_region = jnp.roll(counts[:, :, 2], 1, axis=1)
    from_next_region = jnp.roll(counts[:, :, 3], -1, axis=1)
    received = jnp.stack([from_prev_band, from_next_band, from_prev_region, from_next_region], axis=0)
    draw_keys = jax.random.split(jax.random.fold_in(key, 37), 3)
    grid_shape = (STENCIL, N_BAND, N_REGION, P_DEV)
    own_pick = jax.random.randint(draw_keys[0], grid_shape, 0, P_DEV)
    choose = jax.random.randint(draw_keys[1], grid_shape, 0, 8)
    side_pick = jnp.minimum(choose, 3)
    side_count = jnp.zeros(grid_shape, jnp.int32)
    for direction in range(4):
        side_count = side_count + jnp.where(side_pick == direction, received[direction][None, :, :, None], 0)
    slot_limit = jnp.maximum(side_count, 1) * BLK
    slot_pick = jax.random.randint(draw_keys[2], grid_shape, 0, slot_limit)
    use_halo = (choose < 4) & (side_count > 0)
    source_ids = jnp.where(use_halo, P_DEV + side_pick * (HB * BLK) + slot_pick, own_pick)
    source_ids = source_ids.at[0, 0, (star_region - 1) % N_REGION, 0].set(P_DEV + 4 * HB * BLK - 1)
    source_ids = source_ids.at[1, 0, 0, 0].set(0)
    return source_ids.reshape(STENCIL, N_BAND * N_REGION * P_DEV).astype(jnp.int32)


def draw_vertical_op(key, part):
    diag_key, spread_key = jax.random.split(jax.random.fold_in(key, 5))
    diagonal = jax.random.uniform(diag_key, (LEV,), jnp.float32, 1.0, 2.0)
    spread = jax.random.uniform(spread_key, (LEV, LEV), jnp.float32, -0.4, 0.4)
    level_ids = jnp.arange(LEV)
    distance = jnp.abs(level_ids[:, None] - level_ids[None, :])
    on_diagonal = diagonal[:, None] * jnp.ones((1, LEV), jnp.float32)
    return jnp.where(distance == 0, on_diagonal, jnp.where(distance <= 2, spread, 0.0)).astype(jnp.float32)


def with_ends(drawn, rng, low, largest):
    longest = drawn.shape.index(max(drawn.shape))
    spots = []
    for shift in (0, 1):
        where = [jax.random.randint(jax.random.fold_in(rng, axis), (), 0, length) for axis, length in enumerate(drawn.shape)]
        where[longest] = (where[longest] + shift) % drawn.shape[longest]
        spots.append(tuple(where))
    return drawn.at[spots[0]].set(low).at[spots[1]].set(largest)


def block_levels(own_key, shape, cuts, least, top_value):
    def one(dim, blocks):
        steps = jax.random.uniform(jax.random.fold_in(jax.random.fold_in(own_key, 6), dim), (blocks,), jnp.float32, least / len(cuts), top_value / len(cuts))
        return jnp.repeat(jnp.exp(steps), shape[dim] // blocks).reshape((-1,) + (1,) * (len(shape) - dim - 1))

    loudness = one(*cuts[0])
    for cut in cuts[1:]:
        loudness = loudness * one(*cut)
    return loudness


def scatter_about(key, extent, scale, reach, shards=(), kind=jnp.bfloat16):
    entries = scale * jax.random.normal(key, extent, jnp.float32)
    if shards:
        entries = entries * block_levels(key, extent, shards, -0.22, 0.18)
    return jnp.clip(entries, -reach, reach).astype(kind)


def setup_inputs(seed: int = 0) -> dict:
    key_list = jax.random.split(jax.random.key(seed), 8)
    return {
        "fields": scatter_about(key_list[0], (NPTS, FL), 1.0, 6.0, ((0, 32),), jnp.float32),
        "send_list": draw_send_list(jax.random.fold_in(key_list[7], 71), 0),
        "departure": draw_departure(jax.random.fold_in(key_list[7], 71), 0),
        "hweight": jnp.clip(-0.2 + 0.7 * jax.random.uniform(key_list[3], (STENCIL, NPTS), jnp.float32) ** block_levels(key_list[3], (STENCIL, NPTS), ((1, 32),), -0.2, 0.2), -0.2, 0.5),
        "base_level": with_ends(jax.random.randint(key_list[4], (LEV, NPTS), 1, LEV - 2), jax.random.fold_in(key_list[4], 1), 1, (LEV - 2) - 1).astype(jnp.int32),
        "vweight": jnp.clip(-0.25 + 1.0 * jax.random.uniform(key_list[5], (4, LEV, NPTS), jnp.float32) ** block_levels(key_list[5], (4, LEV, NPTS), ((2, 32),), -0.2, 0.2), -0.25, 0.75),
        "vertical_op": draw_vertical_op(jax.random.fold_in(key_list[7], 71), 0),
    }


exact_mode = lax.Precision.HIGHEST


def pack_blocks(block_table, block_list):
    safe_list = jnp.maximum(block_list, 0)
    picked = jnp.take(block_table, safe_list, axis=0)
    keeping = (block_list >= 0)[:, None, None]
    picked = jnp.where(keeping, picked, jnp.zeros((), picked.dtype))
    return picked.reshape(-1, picked.shape[-1])


def column_update(extended, depart_block, hweight_block, base_block, vweight_block, vertical_op):
    stencil_len, point_count = depart_block.shape
    width_all = extended.shape[1]
    levels = vertical_op.shape[0]
    fields_count = width_all // levels
    picked = jnp.take(extended, depart_block.reshape(-1), axis=0).reshape(stencil_len, point_count, width_all)
    horizontal = jnp.sum(hweight_block[:, :, None] * picked, axis=0)
    stacked = jnp.transpose(horizontal).reshape(fields_count, levels, point_count)
    interpolated = jnp.zeros(stacked.shape, jnp.float32)
    for offset in range(4):
        chosen = jnp.broadcast_to((base_block + (offset - 1))[None, :, :], stacked.shape)
        picked_levels = jnp.take_along_axis(stacked, chosen, axis=1)
        interpolated = interpolated + vweight_block[offset][None, :, :] * picked_levels
    operated = jnp.einsum("kl,flp->fkp", vertical_op, interpolated, precision=exact_mode)
    return operated.reshape(width_all, point_count)


def reference(fields, send_list, departure, hweight, base_level, vweight, vertical_op):
    width_all = fields.shape[1]
    block_count = P_DEV // BLK
    step_points = min(256, P_DEV)

    def device_blocks(device_id):
        start_row = (device_id * P_DEV).astype(jnp.int32)
        return lax.dynamic_slice_in_dim(fields, start_row, P_DEV, 0).reshape(block_count, BLK, width_all)

    def one_device(device_id):
        band_id = device_id // N_REGION
        region_id = device_id % N_REGION
        prev_band = jnp.maximum(band_id - 1, 0)
        next_band = jnp.minimum(band_id + 1, N_BAND - 1)
        prev_region = (region_id - 1) % N_REGION
        next_region = (region_id + 1) % N_REGION
        from_north = pack_blocks(device_blocks(prev_band * N_REGION + region_id), send_list[prev_band, region_id, 0])
        from_north = jnp.where(band_id > 0, from_north, jnp.zeros((), from_north.dtype))
        from_south = pack_blocks(device_blocks(next_band * N_REGION + region_id), send_list[next_band, region_id, 1])
        from_south = jnp.where(band_id < N_BAND - 1, from_south, jnp.zeros((), from_south.dtype))
        from_west = pack_blocks(device_blocks(band_id * N_REGION + prev_region), send_list[band_id, prev_region, 2])
        from_east = pack_blocks(device_blocks(band_id * N_REGION + next_region), send_list[band_id, next_region, 3])
        own_rows = device_blocks(device_id).reshape(P_DEV, width_all)
        extended = jnp.concatenate([own_rows, from_north, from_south, from_west, from_east], axis=0)
        base_col = (device_id * P_DEV).astype(jnp.int32)

        def one_step(step_id):
            first_col = (base_col + step_id * step_points).astype(jnp.int32)
            return column_update(
                extended,
                lax.dynamic_slice_in_dim(departure, first_col, step_points, 1),
                lax.dynamic_slice_in_dim(hweight, first_col, step_points, 1),
                lax.dynamic_slice_in_dim(base_level, first_col, step_points, 1),
                lax.dynamic_slice_in_dim(vweight, first_col, step_points, 2),
                vertical_op)

        pieces = lax.map(one_step, jnp.arange(P_DEV // step_points, dtype=jnp.int32))
        return jnp.transpose(pieces, (1, 0, 2)).reshape(width_all, P_DEV)

    results = lax.map(one_device, jnp.arange(N_BAND * N_REGION, dtype=jnp.int32))
    return jnp.transpose(results, (1, 0, 2)).reshape(width_all, N_BAND * N_REGION * P_DEV)
```

```python
import jax
import jax.numpy as jnp
from jax import lax
from jax.experimental import pallas as pl
from jax.experimental.pallas import tpu as pltpu
from jax.sharding import PartitionSpec as P

BLK = 128
LANES = 128

VMEM = pltpu.MemorySpace.VMEM
SMEM = pltpu.MemorySpace.SMEM


def split(x):
    hi = x.astype(jnp.bfloat16)
    lo = (x - hi.astype(jnp.float32)).astype(jnp.bfloat16)
    return hi, lo


def mm(a, b, dims):
    return lax.dot_general(a, b, (dims, ((), ())), preferred_element_type=jnp.float32)


def mm3(a, b, dims):
    (ah, al), (bh, bl) = a, b
    return mm(ah, bh, dims) + (mm(ah, bl, dims) + mm(al, bh, dims))


def prep_kernel(
    own_blocks, list_len, ids, lists, dep, hw, base, vw, w_hi, w_lo, idx_out, vwt_out
):
    stencil, points = dep.shape
    list_blocks = 4 * list_len
    d = dep[...]
    block = d // BLK
    renamed = block
    for j in range(list_blocks):
        direction, slot = divmod(j, list_len)
        at = ids[direction] * list_blocks + direction * list_len + slot
        target = own_blocks * (1 + direction) + jnp.maximum(lists[at], 0)
        renamed = jnp.where(block == own_blocks + j, target, renamed)
    rows = renamed * BLK + (d - block * BLK)
    pad = LANES - stencil
    rows_t = jnp.concatenate([rows, jnp.zeros((pad, points), jnp.int32)], axis=0).T
    hw_t = jnp.concatenate([hw[...], jnp.zeros((pad, points), jnp.float32)], axis=0).T
    lane = lax.broadcasted_iota(jnp.int32, (points, LANES), 1)
    total = w_hi.shape[1]
    for j in range(total // LANES):
        acc = jnp.zeros((points, LANES), jnp.float32)
        for c in range(stencil):
            hit = (rows_t[:, c : c + 1] - j * LANES) == lane
            acc = acc + jnp.where(hit, hw_t[:, c : c + 1], 0.0)
        hi, lo = split(acc)
        w_hi[:, j * LANES : (j + 1) * LANES] = hi
        w_lo[:, j * LANES : (j + 1) * LANES] = lo
    idx_out[...] = base[...].T
    for m in range(4):
        vwt_out[m] = vw[m].T


def main_kernel(w_hi, w_lo, own, north, south, west, east, idx, vwt, op, out, hor, inter):
    points = own.shape[0]
    levels = op.shape[0]
    for i, part in enumerate((own, north, south, west, east)):
        cols = slice(i * points, (i + 1) * points)
        got = mm3((w_hi[:, cols], w_lo[:, cols]), split(part[...]), ((1,), (0,)))
        if i == 0:
            hor[...] = got
        else:
            hor[...] += got
    op_parts = split(op[...])
    for f in range(own.shape[1] // levels):
        cols = slice(f * levels, (f + 1) * levels)
        h = hor[:, cols]
        acc = jnp.zeros_like(h)
        for m in range(4):
            acc = acc + vwt[m] * jnp.take_along_axis(
                h, idx[...] + (m - 1), axis=1, mode="promise_in_bounds"
            )
        out[cols, :] = mm3(op_parts, split(acc), ((1,), (1,)))


def body(fields, send_list, departure, hweight, base_level, vweight, vertical_op):
    points, width = fields.shape
    levels = vertical_op.shape[0]
    band, region = lax.axis_index("band"), lax.axis_index("region")
    bands, regions = lax.axis_size("band"), lax.axis_size("region")
    list_len = send_list.shape[3]

    def shift(axis, size, step, wrap):
        if wrap:
            route = [((i - step) % size, i) for i in range(size)]
        else:
            route = [(i - step, i) for i in range(size) if 0 <= i - step < size]
        return lax.ppermute(fields, axis, route)

    north = shift("band", bands, 1, False)
    south = shift("band", bands, -1, False)
    west = shift("region", regions, 1, True)
    east = shift("region", regions, -1, True)
    senders = jnp.stack(
        [
            jnp.maximum(band - 1, 0) * regions + region,
            jnp.minimum(band + 1, bands - 1) * regions + region,
            band * regions + (region - 1) % regions,
            band * regions + (region + 1) % regions,
        ]
    ).astype(jnp.int32)
    f32, bf16 = jnp.float32, jnp.bfloat16
    total = 5 * points
    vm = pl.BlockSpec(memory_space=VMEM)
    sm = pl.BlockSpec(memory_space=SMEM)
    w_hi, w_lo, idx, vwt = pl.pallas_call(
        lambda *refs: prep_kernel(points // BLK, list_len, *refs),
        out_shape=(
            jax.ShapeDtypeStruct((points, total), bf16),
            jax.ShapeDtypeStruct((points, total), bf16),
            jax.ShapeDtypeStruct((points, levels), jnp.int32),
            jax.ShapeDtypeStruct((4, points, levels), f32),
        ),
        in_specs=[sm, sm, vm, vm, vm, vm],
        out_specs=(vm, vm, vm, vm),
        name="prep",
    )(senders, send_list.reshape(-1), departure, hweight, base_level, vweight)
    result = pl.pallas_call(
        main_kernel,
        out_shape=jax.ShapeDtypeStruct((width, points), f32),
        in_specs=[vm] * 10,
        out_specs=vm,
        scratch_shapes=[pltpu.VMEM((points, width), f32), pltpu.VMEM((points, levels), f32)],
        name="interp",
    )(w_hi, w_lo, fields, north, south, west, east, idx, vwt, vertical_op)
    return lax.all_to_all(result, "region", split_axis=0, concat_axis=1, tiled=True)


def solution(mesh):
    placed = (
        P(("band", "region"), None),
        P(),
        P(None, ("band", "region")),
        P(None, ("band", "region")),
        P(None, ("band", "region")),
        P(None, None, ("band", "region")),
        P(),
    )
    return jax.shard_map(
        body, mesh=mesh, in_specs=placed, out_specs=P("region", "band"), check_vma=False
    )
```

```python
import jax
import jax.numpy as jnp
from jax import lax
from jax.experimental import pallas as pl
from jax.experimental.pallas import tpu as pltpu
from jax.sharding import PartitionSpec as P

BLK = 128
LANES = 128
STRIP = 16

VMEM = pltpu.MemorySpace.VMEM
SMEM = pltpu.MemorySpace.SMEM


def split(x):
    hi = x.astype(jnp.bfloat16)
    lo = (x - hi.astype(jnp.float32)).astype(jnp.bfloat16)
    return hi, lo


def mm(a, b, dims):
    return lax.dot_general(a, b, (dims, ((), ())), preferred_element_type=jnp.float32)


def mm3(a, b, dims):
    (ah, al), (bh, bl) = a, b
    return mm(ah, bh, dims) + (mm(ah, bl, dims) + mm(al, bh, dims))


def prep_kernel(
    own_blocks, list_len, ids, lists, dep, hw, base, vw, w_hi, w_lo, idx_out, vwt_out
):
    stencil, points = dep.shape
    list_blocks = 4 * list_len
    d = dep[...]
    block = d // BLK
    renamed = block
    for j in range(list_blocks):
        direction, slot = divmod(j, list_len)
        at = ids[direction] * list_blocks + direction * list_len + slot
        target = own_blocks * (1 + direction) + jnp.maximum(lists[at], 0)
        renamed = jnp.where(block == own_blocks + j, target, renamed)
    rows = renamed * BLK + (d - block * BLK)
    pad = LANES - stencil
    rows_t = jnp.concatenate([rows, jnp.zeros((pad, points), jnp.int32)], axis=0).T
    hw_t = jnp.concatenate([hw[...], jnp.zeros((pad, points), jnp.float32)], axis=0).T
    tiles = w_hi.shape[1] // LANES
    lane = lax.broadcasted_iota(jnp.int32, (STRIP, LANES), 1)
    for p in range(0, points, STRIP):
        strip = slice(p, p + STRIP)
        acc = [jnp.zeros((STRIP, LANES), jnp.float32) for _ in range(tiles)]
        for c in range(stencil):
            row = jnp.broadcast_to(rows_t[strip, c : c + 1], (STRIP, LANES)) - lane
            weight = jnp.broadcast_to(hw_t[strip, c : c + 1], (STRIP, LANES))
            for j in range(tiles):
                acc[j] = acc[j] + jnp.where(row == j * LANES, weight, 0.0)
        for j in range(tiles):
            cols = slice(j * LANES, (j + 1) * LANES)
            w_hi[strip, cols], w_lo[strip, cols] = split(acc[j])
    idx_out[...] = base[...].T
    for m in range(4):
        vwt_out[m] = vw[m].T


def main_kernel(w_hi, w_lo, own, north, south, west, east, idx, vwt, op, out, hor):
    points = own.shape[0]
    levels = op.shape[0]
    for i, part in enumerate((own, north, south, west, east)):
        cols = slice(i * points, (i + 1) * points)
        got = mm3((w_hi[:, cols], w_lo[:, cols]), split(part[...]), ((1,), (0,)))
        if i == 0:
            hor[...] = got
        else:
            hor[...] += got
    op_parts = split(op[...])
    for f in range(own.shape[1] // levels):
        cols = slice(f * levels, (f + 1) * levels)
        h = hor[:, cols]
        acc = jnp.zeros_like(h)
        for m in range(4):
            acc = acc + vwt[m] * jnp.take_along_axis(
                h, idx[...] + (m - 1), axis=1, mode="promise_in_bounds"
            )
        out[cols, :] = mm3(op_parts, split(acc), ((1,), (1,)))


def body(fields, send_list, departure, hweight, base_level, vweight, vertical_op):
    points, width = fields.shape
    levels = vertical_op.shape[0]
    band, region = lax.axis_index("band"), lax.axis_index("region")
    bands, regions = lax.axis_size("band"), lax.axis_size("region")
    list_len = send_list.shape[3]

    def shift(axis, size, step, wrap):
        if wrap:
            route = [((i - step) % size, i) for i in range(size)]
        else:
            route = [(i - step, i) for i in range(size) if 0 <= i - step < size]
        return lax.ppermute(fields, axis, route)

    north = shift("band", bands, 1, False)
    south = shift("band", bands, -1, False)
    west = shift("region", regions, 1, True)
    east = shift("region", regions, -1, True)
    senders = jnp.stack(
        [
            jnp.maximum(band - 1, 0) * regions + region,
            jnp.minimum(band + 1, bands - 1) * regions + region,
            band * regions + (region - 1) % regions,
            band * regions + (region + 1) % regions,
        ]
    ).astype(jnp.int32)
    f32, bf16 = jnp.float32, jnp.bfloat16
    total = 5 * points
    vm = pl.BlockSpec(memory_space=VMEM)
    sm = pl.BlockSpec(memory_space=SMEM)
    w_hi, w_lo, idx, vwt = pl.pallas_call(
        lambda *refs: prep_kernel(points // BLK, list_len, *refs),
        out_shape=(
            jax.ShapeDtypeStruct((points, total), bf16),
            jax.ShapeDtypeStruct((points, total), bf16),
            jax.ShapeDtypeStruct((points, levels), jnp.int32),
            jax.ShapeDtypeStruct((4, points, levels), f32),
        ),
        in_specs=[sm, sm, vm, vm, vm, vm],
        out_specs=(vm, vm, vm, vm),
        compiler_params=pltpu.CompilerParams(vmem_limit_bytes=8 << 20),
        name="prep",
    )(senders, send_list.reshape(-1), departure, hweight, base_level, vweight)
    result = pl.pallas_call(
        main_kernel,
        out_shape=jax.ShapeDtypeStruct((width, points), f32),
        in_specs=[vm] * 10,
        out_specs=vm,
        scratch_shapes=[pltpu.VMEM((points, width), f32)],
        compiler_params=pltpu.CompilerParams(vmem_limit_bytes=8 << 20),
        name="interp",
    )(w_hi, w_lo, fields, north, south, west, east, idx, vwt, vertical_op)
    return lax.all_to_all(result, "region", split_axis=0, concat_axis=1, tiled=True)


def solution(mesh):
    placed = (
        P(("band", "region"), None),
        P(),
        P(None, ("band", "region")),
        P(None, ("band", "region")),
        P(None, ("band", "region")),
        P(None, None, ("band", "region")),
        P(),
    )
    return jax.shard_map(
        body, mesh=mesh, in_specs=placed, out_specs=P("region", "band"), check_vma=False
    )
```
